1024 devices in a mesh: dp: 64 (over z, x_lo, core), tensor: 16 (over x_hi, y).
Axes of the slice: x: 4 (x_hi: 2, x_lo: 2; x = x_hi * 2 + x_lo), y: 8, z: 16, core: 2. Of those that a mesh axis runs over, the one named last changes fastest.
Arguments:
- latent_pre: bfloat16 [32768, 512], P('dp'), may hold values from -16 to 16
- norm_gain: float32 [512], replicated, may hold values from 0.1 to 1.9
- kv_weight: bfloat16 [512, 32768], P(None, 'tensor'), may hold values from -0.25 to 0.25
- down_weight: bfloat16 [7168, 512], P('tensor'), may hold values from -0.25 to 0.25
- grad_kv: bfloat16 [32768, 32768], P('dp', 'tensor'), may hold values from -0.75 to 0.75
- master: float32 [512, 32768], P('dp', 'tensor'), may hold values from -0.25 to 0.25
- first_moment: float32 [512, 32768], P('dp', 'tensor'), may hold values from -120 to 120
- second_moment: float32 [512, 32768], P('dp', 'tensor'), may hold values from 100 to 1000
Outputs:
- grad_hidden: bfloat16 [32768, 7168], P('dp', 'tensor')
- new_master: float32 [512, 32768], P('dp', 'tensor')
- new_first: float32 [512, 32768], P('dp', 'tensor')
- new_second: float32 [512, 32768], P('dp', 'tensor')
- new_replica: bfloat16 [512, 32768], P(None, 'tensor')
The draws below stay inside these ranges and needn't reach their ends.
All inputs are finite; a program needn't handle non-finite values.
Results may differ from the reference program's by a relative error of at most 0.002.
The reference program's roundings to bfloat16 on the way (of `normalized` and `grad_pre`) count: a program that leaves them out, or rounds other values in their place, can miss the bound.
Values may be sent and summed in bfloat16 or wider, within the bound.
No kernel may reach another device: no remote copies, remote signals or barrier semaphores. Data moves between devices by JAX's collectives and lax.ppermute only.
A program may use at most 32 MiB of HBM per device.

```python
import math
import jax
import jax.numpy as jnp
from jax import lax

D = 7168
LATENT = 512
KV_COLS = 32768
TOKENS = 32768


def raised(array, key, source, target, shards_of, factor):
    owner, partner = [(jnp.arange(array.shape[axis_at]) // (array.shape[axis_at] // shards_of)).reshape([-1 if axis == axis_at else 1 for axis in range(array.ndim)]) for axis_at in (source, target)]
    chosen = jax.random.permutation(key, shards_of)[partner]
    strong = (owner == chosen) | (owner == (partner + shards_of // 2) % shards_of)
    return jnp.where(strong, factor * array, array)


def shard_levels(stream_key, dims, shards, least, largest):
    def one(axis_at, parts):
        heights = jax.random.uniform(jax.random.fold_in(jax.random.fold_in(stream_key, 6), axis_at), (parts,), jnp.float32, least / len(shards), largest / len(shards))
        return jnp.repeat(jnp.exp(heights), dims[axis_at] // parts).reshape((-1,) + (1,) * (len(dims) - axis_at - 1))

    gain = one(*shards[0])
    for cut in shards[1:]:
        gain = gain * one(*cut)
    return gain


def bell_draw(own_key, shape, width, bound, cuts=(), kind=jnp.bfloat16):
    array = width * jax.random.normal(own_key, shape, jnp.float32)
    if cuts:
        array = array * shard_levels(own_key, shape, cuts, -0.22, 0.18)
    return jnp.clip(array, -bound, bound).astype(kind)


def heavy_noise(key, dims, deviation, most, cuts, heavy, held_as=jnp.bfloat16):
    values = deviation * jax.random.normal(key, dims, jnp.float32)
    if cuts:
        values = values * shard_levels(key, dims, cuts, -0.22, 0.18)
    return jnp.clip(raised(values, jax.random.fold_in(key, 3), *heavy), -most, most).astype(held_as)


def setup_inputs(seed: int = 0) -> dict:
    key_of = jax.random.split(jax.random.key(seed), 9)
    return {
        "latent_pre": heavy_noise(key_of[0], (TOKENS, LATENT), 1.0, 16.0, ((0, 64),), (0, 1, 64, 4.0)),
        "norm_gain": jnp.clip(1.0 + 0.18 * jax.random.normal(key_of[1], (LATENT,), jnp.float32), 0.1, 1.9),
        "kv_weight": bell_draw(key_of[2], (LATENT, KV_COLS), LATENT ** -0.5, 0.25, ((1, 16),)),
        "down_weight": bell_draw(key_of[3], (D, LATENT), LATENT ** -0.5, 0.25, ((0, 16),)),
        "grad_kv": bell_draw(key_of[4], (TOKENS, KV_COLS), 0.125, 0.75, ((0, 64), (1, 16))),
        "master": bell_draw(key_of[5], (LATENT, KV_COLS), LATENT ** -0.5, 0.25, ((0, 64), (1, 16)), jnp.float32),
        "first_moment": bell_draw(key_of[6], (LATENT, KV_COLS), 20.0, 120.0, ((0, 64), (1, 16)), jnp.float32),
        "second_moment": jnp.clip(jnp.exp(math.log(1000.0) - 2.3025851 * jax.random.uniform(key_of[7], (LATENT, KV_COLS), jnp.float32) ** shard_levels(key_of[7], (LATENT, KV_COLS), ((0, 64), (1, 16)), -0.2, 0.2)), 100.0, 1000.0),
    }


bias_first = 0.9999734386011124
bias_second = 0.09520785288629112

def reference(latent_pre, norm_gain, kv_weight, down_weight, grad_kv, master, first_moment, second_moment):
    values = latent_pre.astype(jnp.float32)
    inverse_rms = lax.rsqrt(lax.optimization_barrier(jnp.mean(values * values, axis=1, keepdims=True)) + 1e-06)
    unit = values * inverse_rms
    normalized = (unit * norm_gain).astype(jnp.bfloat16)
    grad_latent = lax.dot_general(grad_kv, kv_weight, (((1,), (1,)), ((), ())), preferred_element_type=jnp.float32)
    scaled = grad_latent * norm_gain
    inner = lax.optimization_barrier(jnp.mean(scaled * unit, axis=1, keepdims=True))
    grad_pre = (inverse_rms * (scaled - unit * inner)).astype(jnp.bfloat16)
    grad_hidden = lax.dot_general(grad_pre, down_weight, (((1,), (1,)), ((), ())), preferred_element_type=jnp.float32).astype(jnp.bfloat16)
    weight_grad = lax.dot_general(normalized, grad_kv, (((0,), (0,)), ((), ())), preferred_element_type=jnp.float32)
    new_first = 0.9 * first_moment + 0.1 * weight_grad
    new_second = 0.999 * second_moment + 0.001 * weight_grad * weight_grad
    first_hat = new_first / bias_first
    second_hat = new_second / bias_second
    new_master = master - 0.01 * (first_hat / (jnp.sqrt(second_hat) + 1e-08) + 0.1 * master)
    return (grad_hidden, new_master, new_first, new_second, new_master.astype(jnp.bfloat16))
```

```python
import jax
import jax.numpy as jnp
from jax import lax
from jax.sharding import Mesh
from jax.sharding import PartitionSpec as P

Z = ("zh", "zl")
TENSOR = ("xh", "y")
DP = ("zh", "zl", "xl", "c")
SWAP = [(0, 1), (1, 0)]

bias_first = 0.9999734386011124
bias_second = 0.09520785288629112

F32 = jnp.float32
BF16 = jnp.bfloat16


def at(x, index, dim):
    return lax.dynamic_index_in_dim(x, index, dim, keepdims=False)


def reduce_pair(x, axis, dim):
    me = lax.axis_index(axis)
    got = lax.ppermute(at(x, 1 - me, dim).astype(BF16), axis, SWAP)
    return at(x, me, dim).astype(F32) + got.astype(F32)


def gather_pair(x, axis, dim):
    me = lax.axis_index(axis)
    got = lax.ppermute(x, axis, SWAP)
    first = jnp.where(me == 0, x, got)
    second = jnp.where(me == 0, got, x)
    return jnp.stack([first, second], axis=dim)


def to_all(x, axis):
    n = lax.axis_size(axis)
    return lax.all_to_all(jnp.broadcast_to(x[None], (n, *x.shape)), axis, 0, 0, tiled=True)


def norm_backward(latent_rows, norm_gain, grad_rows):
    values = latent_rows.astype(F32)
    inverse_rms = lax.rsqrt(jnp.mean(values * values, axis=1, keepdims=True) + 1e-06)
    unit = values * inverse_rms
    scaled = grad_rows * norm_gain
    inner = jnp.mean(scaled * unit, axis=1, keepdims=True)
    return (inverse_rms * (scaled - unit * inner)).astype(BF16)


def local(
    latent_pre, norm_gain, kv_weight, down_weight, grad_kv, master, first_moment, second_moment
):
    values = latent_pre.astype(F32)
    inverse_rms = lax.rsqrt(jnp.mean(values * values, axis=1, keepdims=True) + 1e-06)
    normalized = (values * inverse_rms * norm_gain).astype(BF16)
    cols = grad_kv.shape[1]
    half = cols // 2
    zh, zl, xl, c = (lax.axis_size(a) for a in DP)
    part = lax.dot_general(
        normalized, grad_kv, (((0,), (0,)), ((), ())), preferred_element_type=F32
    )
    rows = part.shape[0] // (zh * zl * xl * c)
    part = part.reshape(zh, zl, xl, c, rows, cols)
    part = reduce_pair(part, "c", 3)
    grad_part = lax.dot_general(
        grad_kv, kv_weight, (((1,), (1,)), ((), ())), preferred_element_type=F32
    )
    share = grad_part.shape[0] // lax.axis_size(TENSOR)
    blocks = lax.all_to_all(
        grad_part.reshape(-1, share, grad_part.shape[1]), TENSOR, 0, 0, tiled=True
    )
    grad_share = jnp.sum(blocks, axis=0)
    own_start = lax.axis_index(TENSOR) * share
    latent_share = lax.dynamic_slice_in_dim(latent_pre, own_start, share, 0)
    pre_share = norm_backward(latent_share, norm_gain, grad_share)
    grad_pre = to_all(pre_share, TENSOR).reshape(latent_pre.shape)
    grad_hidden = lax.dot_general(
        grad_pre, down_weight, (((1,), (1,)), ((), ())), preferred_element_type=F32
    ).astype(BF16)
    p = part[..., :half]
    q = part[..., half:]
    p = reduce_pair(p, "xl", 2)
    q = reduce_pair(q, "zl", 1)
    p = reduce_pair(p, "zl", 1)
    q = reduce_pair(q, "xl", 1)
    both = jnp.concatenate([p.astype(BF16), q.astype(BF16)], axis=-1)
    both = lax.all_to_all(both, "zh", 0, 0, tiled=True)
    weight_grad = jnp.sum(both.astype(F32), axis=0)
    new_first = 0.9 * first_moment + 0.1 * weight_grad
    new_second = 0.999 * second_moment + 0.001 * weight_grad * weight_grad
    first_hat = new_first / bias_first
    second_hat = new_second / bias_second
    new_master = master - 0.01 * (first_hat / (jnp.sqrt(second_hat) + 1e-08) + 0.1 * master)
    rep = to_all(new_master.astype(BF16), "zh")
    p = gather_pair(rep[..., :half], "zl", 1)
    q = gather_pair(rep[..., half:], "xl", 1)
    p = gather_pair(p, "xl", 2)
    q = gather_pair(q, "zl", 1)
    both = jnp.concatenate([p, q], axis=-1)
    new_replica = gather_pair(both, "c", 3).reshape(-1, cols)
    return (grad_hidden, new_master, new_first, new_second, new_replica)


def solution(mesh):
    torus = Mesh(mesh.devices.reshape(8, 2, 2, 2, 2, 8), ("zh", "zl", "xl", "c", "xh", "y"))
    placed = (
        P(DP, None),
        P(),
        P(None, TENSOR),
        P(TENSOR, None),
        P(DP, TENSOR),
        P(DP, TENSOR),
        P(DP, TENSOR),
        P(DP, TENSOR),
    )
    return jax.shard_map(
        local,
        mesh=torus,
        in_specs=placed,
        out_specs=(P(DP, TENSOR), P(DP, TENSOR), P(DP, TENSOR), P(DP, TENSOR), P(None, TENSOR)),
        check_vma=False,
    )
```

```python
import jax
import jax.numpy as jnp
from jax import lax
from jax.experimental import pallas as pl
from jax.experimental.pallas import tpu as pltpu
from jax.sharding import Mesh
from jax.sharding import PartitionSpec as P

TENSOR = ("xh", "y2", "y1", "y0")
DP = ("zh", "zl", "xl", "c")
SWAP = [(0, 1), (1, 0)]

bias_first = 0.9999734386011124
bias_second = 0.09520785288629112

F32 = jnp.float32
BF16 = jnp.bfloat16
VMEM = pltpu.VMEM


def shaped(shape, dtype):
    return jax.ShapeDtypeStruct(shape, dtype)


def pick(second, first_value, second_value):
    return jnp.where(second, second_value, first_value)


def weight_gradient_kernel(ids, latent, gain, grad, send, own, turned):
    @pl.when(pl.program_id(0) == 0)
    def _():
        values = latent[...].astype(F32)
        inverse_rms = lax.rsqrt(jnp.mean(values * values, axis=1, keepdims=True) + 1e-06)
        turned[...] = (values * inverse_rms * gain[...]).T.astype(BF16)

    part = lax.dot_general(
        turned[...], grad[...], (((1,), (0,)), ((), ())), preferred_element_type=F32
    )
    rows, cols = part.shape
    part = part.reshape(rows // 16, 2, 8, cols)
    one = ids[2] == 1
    own[...] = pick(one, part[:, 0], part[:, 1]).reshape(rows // 2, cols)
    send[...] = pick(one, part[:, 1], part[:, 0]).reshape(rows // 2, cols).astype(BF16)


def weight_gradient(ids, latent, gain, grad):
    tokens, latents = latent.shape
    cols = grad.shape[1]
    block = 512
    return pl.pallas_call(
        weight_gradient_kernel,
        grid=(cols // block,),
        in_specs=[
            pl.BlockSpec(memory_space=pltpu.SMEM),
            pl.BlockSpec((tokens, latents), lambda j: (0, 0)),
            pl.BlockSpec((1, latents), lambda j: (0, 0)),
            pl.BlockSpec((tokens, block), lambda j: (0, j)),
        ],
        out_specs=[
            pl.BlockSpec((latents // 2, block), lambda j: (0, j)),
            pl.BlockSpec((latents // 2, block), lambda j: (0, j)),
        ],
        out_shape=[shaped((latents // 2, cols), BF16), shaped((latents // 2, cols), F32)],
        scratch_shapes=[VMEM((latents, tokens), BF16)],
        name="weight_gradient",
    )(ids, latent, gain, grad)


def first_split_kernel(ids, own, got, p_send, p_own, q_send, q_own):
    total = own[...] + got[...].astype(F32)
    rows, cols = total.shape
    half = cols // 2
    total = total.reshape(rows // 32, 2, 2, 8, cols)
    p = total[..., :half]
    q = total[..., half:]
    zl = ids[0] == 1
    xl = ids[1] == 1
    flat = (rows // 2, half)
    p_own[...] = pick(xl, p[:, :, 0], p[:, :, 1]).reshape(flat)
    p_send[...] = pick(xl, p[:, :, 1], p[:, :, 0]).reshape(flat).astype(BF16)
    q_own[...] = pick(zl, q[:, 0], q[:, 1]).reshape(flat)
    q_send[...] = pick(zl, q[:, 1], q[:, 0]).reshape(flat).astype(BF16)


def first_split(ids, own, got):
    rows, cols = own.shape
    half = cols // 2
    block = rows // 4
    row_block = lambda r, n: pl.BlockSpec((r, n), lambda i: (i, 0))
    return pl.pallas_call(
        first_split_kernel,
        grid=(rows // block,),
        in_specs=[pl.BlockSpec(memory_space=pltpu.SMEM), row_block(block, cols), row_block(block, cols)],
        out_specs=[row_block(block // 2, half)] * 4,
        out_shape=[shaped((rows // 2, half), BF16), shaped((rows // 2, half), F32)] * 2,
        name="first_split",
    )(ids, own, got)


def second_split_kernel(which, ids, own, got, send, keep):
    total = own[...] + got[...].astype(F32)
    rows, cols = total.shape
    total = total.reshape(rows // 16, 2, 8, cols)
    one = ids[which] == 1
    keep[...] = pick(one, total[:, 0], total[:, 1]).reshape(rows // 2, cols)
    send[...] = pick(one, total[:, 1], total[:, 0]).reshape(rows // 2, cols).astype(BF16)


def second_split(ids, which, own, got):
    rows, cols = own.shape
    return pl.pallas_call(
        lambda *refs: second_split_kernel(which, *refs),
        in_specs=[pl.BlockSpec(memory_space=pltpu.SMEM)] + [pl.BlockSpec(memory_space=VMEM)] * 2,
        out_specs=[pl.BlockSpec(memory_space=VMEM)] * 2,
        out_shape=[shaped((rows // 2, cols), BF16), shaped((rows // 2, cols), F32)],
        name="second_split",
    )(ids, own, got)


def join_kernel(p_own, p_got, q_own, q_got, out):
    half = p_own.shape[1]
    out[:, :half] = (p_own[...] + p_got[...].astype(F32)).astype(BF16)
    out[:, half:] = (q_own[...] + q_got[...].astype(F32)).astype(BF16)


def join(p_own, p_got, q_own, q_got):
    rows, half = p_own.shape
    return pl.pallas_call(
        join_kernel,
        in_specs=[pl.BlockSpec(memory_space=VMEM)] * 4,
        out_specs=pl.BlockSpec(memory_space=VMEM),
        out_shape=shaped((rows, 2 * half), BF16),
        name="join",
    )(p_own, p_got, q_own, q_got)


def adam_kernel(blocks, master, first, second, new_master, new_first, new_second, copies):
    count = blocks.shape[0] // master.shape[0]
    parts = blocks[...].astype(F32)
    parts = parts.reshape(count, *master.shape)
    weight_grad = jnp.sum(parts, axis=0)
    m1 = 0.9 * first[...] + 0.1 * weight_grad
    m2 = 0.999 * second[...] + 0.001 * weight_grad * weight_grad
    new_first[...] = m1
    new_second[...] = m2
    held = master[...]
    updated = held - 0.01 * (
        (m1 / bias_first) / (jnp.sqrt(m2 / bias_second) + 1e-08) + 0.1 * held
    )
    new_master[...] = updated
    copies[...] = jnp.broadcast_to(updated[None], (count, *updated.shape)).reshape(
        copies.shape
    ).astype(BF16)


def adam(blocks, master, first, second):
    vmem = pl.BlockSpec(memory_space=VMEM)
    return pl.pallas_call(
        adam_kernel,
        in_specs=[vmem] * 4,
        out_specs=[vmem] * 4,
        out_shape=[shaped(master.shape, F32)] * 3 + [shaped(blocks.shape, BF16)],
        name="adam",
    )(blocks, master, first, second)


def copy_all(pairs, sems):
    copies = [pltpu.make_async_copy(a, b, sems.at[k]) for k, (a, b) in enumerate(pairs)]
    for copy in copies:
        copy.start()
    for copy in copies:
        copy.wait()


def replica_kernel(ids, *refs):
    pieces, out, sems = refs[:10], refs[10], refs[11]
    zl, xl, c = ids[0], ids[1], ids[2]
    half = out.shape[-1] // 2
    pairs = []
    for k in range(2):
        rep, rz, rx, dp, dq = pieces[5 * k : 5 * k + 5]
        core = c if k == 0 else 1 - c
        pairs.append((rep, out.at[:, zl, xl, core]))
        pairs.append((rz, out.at[:, 1 - zl, xl, core]))
        pairs.append((rx, out.at[:, zl, 1 - xl, core]))
        pairs.append((dp, out.at[:, 1 - zl, 1 - xl, core, :, pl.ds(0, half)]))
        pairs.append((dq, out.at[:, 1 - zl, 1 - xl, core, :, pl.ds(half, half)]))
    copy_all(pairs, sems)


def place_replica(ids, pieces):
    zh, rows, cols = pieces[0].shape
    anywhere = pl.BlockSpec(memory_space=pl.ANY)
    return pl.pallas_call(
        replica_kernel,
        in_specs=[pl.BlockSpec(memory_space=pltpu.SMEM)] + [anywhere] * 10,
        out_specs=anywhere,
        out_shape=shaped((zh, 2, 2, 2, rows, cols), BF16),
        scratch_shapes=[pltpu.SemaphoreType.DMA((10,))],
        name="place_replica",
    )(ids, *pieces)


def tokens_kernel(ids, own, xh, y2, y1, y0, out, sems):
    me = ids[3]
    pairs = [(own.at[0], out.at[me]), (xh.at[0], out.at[me ^ 8])]
    for k in range(2):
        pairs.append((y2.at[k], out.at[me ^ (4 | 8 * k)]))
    for k in range(4):
        pairs.append((y1.at[k], out.at[me ^ (2 | 8 * (k & 1) | 4 * (k >> 1))]))
    for k in range(8):
        pairs.append((y0.at[k], out.at[me ^ (1 | 8 * (k & 1) | 4 * (k >> 1 & 1) | 2 * (k >> 2))]))
    copy_all(pairs, sems)


def place_tokens(ids, *pieces):
    anywhere = pl.BlockSpec(memory_space=pl.ANY)
    return pl.pallas_call(
        tokens_kernel,
        in_specs=[pl.BlockSpec(memory_space=pltpu.SMEM)] + [anywhere] * 5,
        out_specs=anywhere,
        out_shape=shaped((16, *pieces[0].shape[1:]), BF16),
        scratch_shapes=[pltpu.SemaphoreType.DMA((16,))],
        name="place_tokens",
    )(ids, *pieces)


def swap(x, axis):
    return lax.ppermute(x, axis, SWAP)


def norm_backward(latent_rows, norm_gain, grad_rows):
    values = latent_rows.astype(F32)
    inverse_rms = lax.rsqrt(jnp.mean(values * values, axis=1, keepdims=True) + 1e-06)
    unit = values * inverse_rms
    scaled = grad_rows * norm_gain
    inner = jnp.mean(scaled * unit, axis=1, keepdims=True)
    return (inverse_rms * (scaled - unit * inner)).astype(BF16)


def local(
    latent_pre, norm_gain, kv_weight, down_weight, grad_kv, master, first_moment, second_moment
):
    barrier = lax.optimization_barrier
    cols = grad_kv.shape[1]
    half = cols // 2
    own_place = lax.axis_index(TENSOR)
    ids = jnp.stack([lax.axis_index(a) for a in ("zl", "xl", "c")] + [own_place]).astype(jnp.int32)
    send, own = weight_gradient(ids, latent_pre, norm_gain[None], grad_kv)
    got = swap(send, "c")
    grad_kv_after, _ = barrier((grad_kv, send))
    grad_part = lax.dot_general(
        grad_kv_after, kv_weight, (((1,), (1,)), ((), ())), preferred_element_type=F32
    )
    share = grad_part.shape[0] // lax.axis_size(TENSOR)
    blocks = lax.all_to_all(
        grad_part.reshape(-1, share, grad_part.shape[1]), TENSOR, 0, 0, tiled=True
    )
    p_send, p_own, q_send, q_own = first_split(ids, own, got)
    p_got = swap(p_send, "xl")
    q_got = swap(q_send, "zl")
    p_send, p_own = second_split(ids, 0, p_own, p_got)
    q_send, q_own = second_split(ids, 1, q_own, q_got)
    p_got = swap(p_send, "zl")
    q_got = swap(q_send, "xl")
    both = join(p_own, p_got, q_own, q_got)
    both, blocks = barrier((both, blocks))
    summed = lax.all_to_all(both.reshape(8, -1, cols), "zh", 0, 0, tiled=True)
    grad_share = jnp.sum(blocks, axis=0)
    latent_share = lax.dynamic_slice_in_dim(latent_pre, own_place * share, share, 0)
    t = norm_backward(latent_share, norm_gain, grad_share)[None]
    t_xh = swap(t, "xh")
    summed, t_xh = barrier((summed, t_xh))
    new_master, new_first, new_second, copies = adam(
        summed.reshape(both.shape), master, first_moment, second_moment
    )
    rep = lax.all_to_all(copies.reshape(8, -1, cols), "zh", 0, 0, tiled=True)
    t2 = jnp.concatenate([t, t_xh])
    t_y2 = swap(t2, "y2")
    t4 = jnp.concatenate([t2, t_y2])
    t_y1 = swap(t4, "y1")
    rep, t_y1 = barrier((rep, t_y1))
    rz = swap(rep, "zl")
    rx = swap(rep, "xl")
    t_y0 = swap(jnp.concatenate([t4, t_y1]), "y0")
    rep_c = swap(rep, "c")
    dp = swap(rz[..., :half], "xl")
    dq = swap(rx[..., half:], "zl")
    rz_c = swap(rz, "c")
    rx_c = swap(rx, "c")
    dp_c = swap(dp, "c")
    dq_c = swap(dq, "c")
    grad_pre = place_tokens(ids, t, t_xh, t_y2, t_y1, t_y0).reshape(latent_pre.shape)
    grad_hidden = lax.dot_general(
        grad_pre, down_weight, (((1,), (1,)), ((), ())), preferred_element_type=F32
    ).astype(BF16)
    new_replica = place_replica(
        ids, (rep, rz, rx, dp, dq, rep_c, rz_c, rx_c, dp_c, dq_c)
    ).reshape(-1, cols)
    return (grad_hidden, new_master, new_first, new_second, new_replica)


def solution(mesh):
    torus = Mesh(
        mesh.devices.reshape(8, 2, 2, 2, 2, 2, 2, 2),
        ("zh", "zl", "xl", "c", "xh", "y2", "y1", "y0"),
    )
    placed = (
        P(DP, None),
        P(),
        P(None, TENSOR),
        P(TENSOR, None),
        P(DP, TENSOR),
        P(DP, TENSOR),
        P(DP, TENSOR),
        P(DP, TENSOR),
    )
    return jax.shard_map(
        local,
        mesh=torus,
        in_specs=placed,
        out_specs=(P(DP, TENSOR), P(DP, TENSOR), P(DP, TENSOR), P(DP, TENSOR), P(None, TENSOR)),
        check_vma=False,
    )
```

```python
import jax
import jax.numpy as jnp
from jax import lax
from jax.sharding import Mesh
from jax.sharding import PartitionSpec as P

TENSOR = ("xh", "y")
DP = ("zh", "zl", "xl", "c")
SWAP = [(0, 1), (1, 0)]

bias_first = 0.9999734386011124
bias_second = 0.09520785288629112

F32 = jnp.float32
BF16 = jnp.bfloat16


def at(x, index, dim):
    return lax.dynamic_index_in_dim(x, index, dim, keepdims=False)


def gather_pair(x, axis, dim):
    got = jnp.expand_dims(lax.ppermute(x, axis, SWAP), dim)
    x = jnp.expand_dims(x, dim)
    place = lax.broadcasted_iota(jnp.int32, tuple(2 if d == dim else 1 for d in range(x.ndim)), dim)
    return jnp.where(place == lax.axis_index(axis), x, got)


def to_all(x, axis):
    n = lax.axis_size(axis)
    return lax.all_to_all(jnp.broadcast_to(x[None], (n, *x.shape)), axis, 0, 0, tiled=True)


def norm_backward(latent_rows, norm_gain, grad_rows):
    values = latent_rows.astype(F32)
    inverse_rms = lax.rsqrt(jnp.mean(values * values, axis=1, keepdims=True) + 1e-06)
    unit = values * inverse_rms
    scaled = grad_rows * norm_gain
    inner = jnp.mean(scaled * unit, axis=1, keepdims=True)
    return (inverse_rms * (scaled - unit * inner)).astype(BF16)


def local(
    latent_pre, norm_gain, kv_weight, down_weight, grad_kv, master, first_moment, second_moment
):
    values = latent_pre.astype(F32)
    inverse_rms = lax.rsqrt(jnp.mean(values * values, axis=1, keepdims=True) + 1e-06)
    normalized = (values * inverse_rms * norm_gain).astype(BF16)
    latents = normalized.shape[1]
    cols = grad_kv.shape[1]
    zh, zl, xl, c = (lax.axis_size(a) for a in DP)
    my_zl, my_xl, my_c = (lax.axis_index(a) for a in DP[1:])
    half = zh // 2
    rows = latents // (zh * zl * xl * c)
    grad_part = lax.dot_general(
        grad_kv, kv_weight, (((1,), (1,)), ((), ())), preferred_element_type=F32
    )
    share = grad_part.shape[0] // lax.axis_size(TENSOR)
    blocks = lax.all_to_all(
        grad_part.reshape(-1, share, grad_part.shape[1]), TENSOR, 0, 0, tiled=True
    )
    grad_kv_after, _ = lax.optimization_barrier((grad_kv, grad_part))

    def rows_of(core, dtype):
        place = lax.broadcasted_iota(jnp.int32, (latents // c, latents), 0)
        latent = lax.broadcasted_iota(jnp.int32, (latents // c, latents), 1)
        wanted = (place // rows * c + core) * rows + place % rows
        chosen = lax.dot_general(
            (latent == wanted).astype(BF16),
            normalized,
            (((1,), (1,)), ((), ())),
            preferred_element_type=F32,
        ).astype(BF16)
        part = lax.dot_general(
            chosen, grad_kv_after, (((1,), (0,)), ((), ())), preferred_element_type=F32
        )
        return part.astype(dtype)

    got = lax.ppermute(rows_of(1 - my_c, BF16), "c", SWAP)
    own = rows_of(my_c, F32)

    def piece(x, start, z=None, x_lo=None):
        starts = (start, 0 if z is None else z, 0 if x_lo is None else x_lo, 0, 0)
        sizes = (half, zl if z is None else 1, xl if x_lo is None else 1, rows, cols)
        block = lax.dynamic_slice(x.reshape(zh, zl, xl, rows, cols), starts, sizes)
        return block.reshape(*(n for n in sizes if n > 1)).astype(F32)

    def pair_sum(start, z=None, x_lo=None):
        return piece(own, start, z, x_lo) + piece(got, start, z, x_lo)

    p_got = lax.ppermute(pair_sum(0, None, 1 - my_xl).astype(BF16), "xl", SWAP)
    q_got = lax.ppermute(pair_sum(half, 1 - my_zl, None).astype(BF16), "zl", SWAP)
    p_send = (pair_sum(0, 1 - my_zl, my_xl) + at(p_got, 1 - my_zl, 1).astype(F32)).astype(BF16)
    p_last = lax.ppermute(p_send, "zl", SWAP)
    q_send = (pair_sum(half, my_zl, 1 - my_xl) + at(q_got, 1 - my_xl, 1).astype(F32)).astype(BF16)
    q_last = lax.ppermute(q_send, "xl", SWAP)
    p_last, q_last = lax.optimization_barrier((p_last, q_last))
    p = pair_sum(0, my_zl, my_xl) + at(p_got, my_zl, 1).astype(F32) + p_last.astype(F32)
    q = pair_sum(half, my_zl, my_xl) + at(q_got, my_xl, 1).astype(F32) + q_last.astype(F32)
    p = p.astype(BF16)
    q = q.astype(BF16)
    both = jnp.concatenate([p, q])
    both, blocks = lax.optimization_barrier((both, blocks))
    both = lax.all_to_all(both, "zh", 0, 0, tiled=True)
    grad_share = jnp.sum(blocks, axis=0)
    own_start = lax.axis_index(TENSOR) * share
    latent_share = lax.dynamic_slice_in_dim(latent_pre, own_start, share, 0)
    pre_share = norm_backward(latent_share, norm_gain, grad_share)
    both, pre_share = lax.optimization_barrier((both, pre_share))
    weight_grad = jnp.sum(both.astype(F32), axis=0)
    new_first = 0.9 * first_moment + 0.1 * weight_grad
    new_second = 0.999 * second_moment + 0.001 * weight_grad * weight_grad
    first_hat = new_first / bias_first
    second_hat = new_second / bias_second
    new_master = master - 0.01 * (first_hat / (jnp.sqrt(second_hat) + 1e-08) + 0.1 * master)
    rep = to_all(new_master.astype(BF16), "zh")
    rep, pre_share = lax.optimization_barrier((rep, pre_share))
    p = gather_pair(rep[:half], "zl", 1)
    q = gather_pair(rep[half:], "xl", 1)
    grad_pre = to_all(pre_share, TENSOR).reshape(latent_pre.shape)
    p = gather_pair(p, "xl", 2)
    q = gather_pair(q, "zl", 1)
    grad_hidden = lax.dot_general(
        grad_pre, down_weight, (((1,), (1,)), ((), ())), preferred_element_type=F32
    ).astype(BF16)
    new_replica = gather_pair(jnp.concatenate([p, q]), "c", 3).reshape(-1, cols)
    return (grad_hidden, new_master, new_first, new_second, new_replica)


def solution(mesh):
    torus = Mesh(mesh.devices.reshape(8, 2, 2, 2, 2, 8), ("zh", "zl", "xl", "c", "xh", "y"))
    placed = (
        P(DP, None),
        P(),
        P(None, TENSOR),
        P(TENSOR, None),
        P(DP, TENSOR),
        P(DP, TENSOR),
        P(DP, TENSOR),
        P(DP, TENSOR),
    )
    return jax.shard_map(
        local,
        mesh=torus,
        in_specs=placed,
        out_specs=(P(DP, TENSOR), P(DP, TENSOR), P(DP, TENSOR), P(DP, TENSOR), P(None, TENSOR)),
        check_vma=False,
    )
```

```python
import jax
import jax.numpy as jnp
from jax import lax
from jax.sharding import Mesh
from jax.sharding import PartitionSpec as P


TENSOR = ("xh", "y")
DP = ("zh", "zl", "xl", "c")
SWAP = [(0, 1), (1, 0)]

bias_first = 0.9999734386011124
bias_second = 0.09520785288629112

F32 = jnp.float32
BF16 = jnp.bfloat16


def at(x, index, dim):
    return lax.dynamic_index_in_dim(x, index, dim, keepdims=False)


def gather_pair(x, axis, dim):
    got = jnp.expand_dims(lax.ppermute(x, axis, SWAP), dim)
    x = jnp.expand_dims(x, dim)
    place = lax.broadcasted_iota(jnp.int32, tuple(2 if d == dim else 1 for d in range(x.ndim)), dim)
    return jnp.where(place == lax.axis_index(axis), x, got)


def to_all(x, axis):
    n = lax.axis_size(axis)
    return lax.all_to_all(jnp.broadcast_to(x[None], (n, *x.shape)), axis, 0, 0, tiled=True)


def norm_backward(latent_rows, norm_gain, grad_rows):
    values = latent_rows.astype(F32)
    inverse_rms = lax.rsqrt(jnp.mean(values * values, axis=1, keepdims=True) + 1e-06)
    unit = values * inverse_rms
    scaled = grad_rows * norm_gain
    inner = jnp.mean(scaled * unit, axis=1, keepdims=True)
    return (inverse_rms * (scaled - unit * inner)).astype(BF16)


def local(
    latent_pre, norm_gain, kv_weight, down_weight, grad_kv, master, first_moment, second_moment
):
    values = latent_pre.astype(F32)
    inverse_rms = lax.rsqrt(jnp.mean(values * values, axis=1, keepdims=True) + 1e-06)
    normalized = (values * inverse_rms * norm_gain).astype(BF16)
    latents = normalized.shape[1]
    cols = grad_kv.shape[1]
    zh, zl, xl, c = (lax.axis_size(a) for a in DP)
    my_zl, my_xl, my_c = (lax.axis_index(a) for a in DP[1:])
    half = zh // 2
    rows = latents // (zh * zl * xl * c)

    def rows_of(core):
        place = lax.broadcasted_iota(jnp.int32, (latents // c, latents), 0)
        latent = lax.broadcasted_iota(jnp.int32, (latents // c, latents), 1)
        return latent == (place // rows * c + core) * rows + place % rows

    picks = jnp.concatenate([rows_of(1 - my_c), rows_of(my_c)]).astype(BF16)
    picked = lax.dot_general(
        picks, normalized, (((1,), (1,)), ((), ())), preferred_element_type=F32
    ).astype(BF16)
    picked = lax.optimization_barrier(picked)

    def product(lhs, rhs):
        return lax.dot_general(lhs, rhs, (((1,), (0,)), ((), ())), preferred_element_type=F32)

    send = product(picked[: latents // c], grad_kv).astype(BF16)
    got = lax.ppermute(send, "c", SWAP)
    grad_kv, _ = lax.optimization_barrier((grad_kv, send))
    grad_part = lax.dot_general(
        grad_kv, kv_weight, (((1,), (1,)), ((), ())), preferred_element_type=F32
    )
    pair = grad_part.shape[0] // lax.axis_size("y")
    share = pair // lax.axis_size("xh")
    blocks = lax.all_to_all(
        grad_part.reshape(-1, pair, grad_part.shape[1]), "y", 0, 0, tiled=True
    )
    grad_kv, _ = lax.optimization_barrier((grad_kv, grad_part))
    own = product(picked[latents // c :], grad_kv)

    def piece(x, start, z=None, x_lo=None):
        starts = (start, 0 if z is None else z, 0 if x_lo is None else x_lo, 0, 0)
        sizes = (half, zl if z is None else 1, xl if x_lo is None else 1, rows, cols)
        block = lax.dynamic_slice(x.reshape(zh, zl, xl, rows, cols), starts, sizes)
        return block.reshape(*(n for n in sizes if n > 1)).astype(F32)

    def pair_sum(start, z=None, x_lo=None):
        return piece(own, start, z, x_lo) + piece(got, start, z, x_lo)

    p_got = lax.ppermute(pair_sum(0, None, 1 - my_xl).astype(BF16), "xl", SWAP)
    q_got = lax.ppermute(pair_sum(half, 1 - my_zl, None).astype(BF16), "zl", SWAP)
    p_send = (pair_sum(0, 1 - my_zl, my_xl) + at(p_got, 1 - my_zl, 1).astype(F32)).astype(BF16)
    p_last = lax.ppermute(p_send, "zl", SWAP)
    q_send = (pair_sum(half, my_zl, 1 - my_xl) + at(q_got, 1 - my_xl, 1).astype(F32)).astype(BF16)
    q_last = lax.ppermute(q_send, "xl", SWAP)
    p_last, q_last = lax.optimization_barrier((p_last, q_last))
    p = pair_sum(0, my_zl, my_xl) + at(p_got, my_zl, 1).astype(F32) + p_last.astype(F32)
    q = pair_sum(half, my_zl, my_xl) + at(q_got, my_xl, 1).astype(F32) + q_last.astype(F32)
    p = p.astype(BF16)
    q = q.astype(BF16)
    both = jnp.concatenate([p, q])
    both, blocks = lax.optimization_barrier((both, blocks))
    both = lax.all_to_all(both, "zh", 0, 0, tiled=True)
    grad_pair = jnp.sum(blocks, axis=0).reshape(-1, share, blocks.shape[2])
    my_xh = lax.axis_index("xh")
    grad_share = at(grad_pair, my_xh, 0) + lax.ppermute(at(grad_pair, 1 - my_xh, 0), "xh", SWAP)
    own_start = lax.axis_index("y") * pair + my_xh * share
    latent_share = lax.dynamic_slice_in_dim(latent_pre, own_start, share, 0)
    pre_share = norm_backward(latent_share, norm_gain, grad_share)
    both, pre_share = lax.optimization_barrier((both, pre_share))
    weight_grad = jnp.sum(both.astype(F32), axis=0)
    new_first = 0.9 * first_moment + 0.1 * weight_grad
    new_second = 0.999 * second_moment + 0.001 * weight_grad * weight_grad
    first_hat = new_first / bias_first
    second_hat = new_second / bias_second
    new_master = master - 0.01 * (first_hat / (jnp.sqrt(second_hat) + 1e-08) + 0.1 * master)
    rep = to_all(new_master.astype(BF16), "zh")
    pre_pair = gather_pair(pre_share, "xh", 0).reshape(pair, -1)
    rep, pre_pair = lax.optimization_barrier((rep, pre_pair))
    p = gather_pair(rep[:half], "zl", 1)
    q = gather_pair(rep[half:], "xl", 1)
    grad_pre = to_all(pre_pair, "y").reshape(latent_pre.shape)
    p = gather_pair(p, "xl", 2)
    q = gather_pair(q, "zl", 1)
    grad_hidden = lax.dot_general(
        grad_pre, down_weight, (((1,), (1,)), ((), ())), preferred_element_type=F32
    ).astype(BF16)
    new_replica = gather_pair(jnp.concatenate([p, q]), "c", 3).reshape(-1, cols)
    return (grad_hidden, new_master, new_first, new_second, new_replica)


def solution(mesh):
    torus = Mesh(mesh.devices.reshape(8, 2, 2, 2, 2, 8), ("zh", "zl", "xl", "c", "xh", "y"))
    placed = (
        P(DP, None),
        P(),
        P(None, TENSOR),
        P(TENSOR, None),
        P(DP, TENSOR),
        P(DP, TENSOR),
        P(DP, TENSOR),
        P(DP, TENSOR),
    )
    return jax.shard_map(
        local,
        mesh=torus,
        in_specs=placed,
        out_specs=(P(DP, TENSOR), P(DP, TENSOR), P(DP, TENSOR), P(DP, TENSOR), P(None, TENSOR)),
        check_vma=False,
    )
```

```python
import jax
import jax.numpy as jnp
from jax import lax
from jax.sharding import Mesh
from jax.sharding import PartitionSpec as P


TENSOR = ("xh", "y")
DP = ("zh", "zl", "xl", "c")
SWAP = [(0, 1), (1, 0)]

bias_first = 0.9999734386011124
bias_second = 0.09520785288629112

F32 = jnp.float32
BF16 = jnp.bfloat16


def at(x, index, dim):
    return lax.dynamic_index_in_dim(x, index, dim, keepdims=False)


def gather_pair(x, axis, dim):
    got = jnp.expand_dims(lax.ppermute(x, axis, SWAP), dim)
    x = jnp.expand_dims(x, dim)
    shape = tuple(2 if d == dim else n for d, n in enumerate(x.shape))
    place = lax.broadcasted_iota(jnp.int32, shape, dim)
    return jnp.where(place == lax.axis_index(axis), x, got)


def to_all(x, axis):
    n = lax.axis_size(axis)
    return lax.all_to_all(jnp.broadcast_to(x[None], (n, *x.shape)), axis, 0, 0, tiled=True)


def norm_backward(latent_rows, norm_gain, grad_rows):
    values = latent_rows.astype(F32)
    inverse_rms = lax.rsqrt(jnp.mean(values * values, axis=1, keepdims=True) + 1e-06)
    unit = values * inverse_rms
    scaled = grad_rows * norm_gain
    inner = jnp.mean(scaled * unit, axis=1, keepdims=True)
    return (inverse_rms * (scaled - unit * inner)).astype(BF16)


def local(
    latent_pre, norm_gain, kv_weight, down_weight, grad_kv, master, first_moment, second_moment
):
    values = latent_pre.astype(F32)
    inverse_rms = lax.rsqrt(jnp.mean(values * values, axis=1, keepdims=True) + 1e-06)
    normalized = (values * inverse_rms * norm_gain).astype(BF16)
    latents = normalized.shape[1]
    cols = grad_kv.shape[1]
    zh, zl, xl, c = (lax.axis_size(a) for a in DP)
    my_zl, my_xl, my_c = (lax.axis_index(a) for a in DP[1:])
    half = zh // 2
    rows = latents // (zh * zl * xl * c)

    def picked_rows(core):
        place = lax.broadcasted_iota(jnp.int32, (latents // c, latents), 0)
        latent = lax.broadcasted_iota(jnp.int32, (latents // c, latents), 1)
        picks = latent == (place // rows * c + core) * rows + place % rows
        picked = lax.dot_general(
            picks.astype(BF16), normalized, (((1,), (1,)), ((), ())), preferred_element_type=F32
        )
        return lax.optimization_barrier(picked.astype(BF16))

    def product(lhs, rhs):
        return lax.dot_general(lhs, rhs, (((1,), (0,)), ((), ())), preferred_element_type=F32)

    send = product(picked_rows(1 - my_c), grad_kv).astype(BF16)
    got = lax.ppermute(send, "c", SWAP)
    grad_kv, _ = lax.optimization_barrier((grad_kv, send))
    grad_part = lax.dot_general(
        grad_kv, kv_weight, (((1,), (1,)), ((), ())), preferred_element_type=F32
    )
    pair = grad_part.shape[0] // lax.axis_size("y")
    share = pair // lax.axis_size("xh")
    blocks = lax.all_to_all(
        grad_part.reshape(-1, pair, grad_part.shape[1]), "y", 0, 0, tiled=True
    )
    grad_kv, my_c, _ = lax.optimization_barrier((grad_kv, my_c, grad_part))
    own = product(picked_rows(my_c), grad_kv)

    def piece(x, start, z=None, x_lo=None):
        starts = (start, 0 if z is None else z, 0 if x_lo is None else x_lo, 0, 0)
        sizes = (half, zl if z is None else 1, xl if x_lo is None else 1, rows, cols)
        block = lax.dynamic_slice(x.reshape(zh, zl, xl, rows, cols), starts, sizes)
        return block.reshape(*(n for n in sizes if n > 1)).astype(F32)

    def pair_sum(start, z=None, x_lo=None):
        return piece(own, start, z, x_lo) + piece(got, start, z, x_lo)

    p_send = pair_sum(0, None, 1 - my_xl).astype(BF16)
    p_got = lax.ppermute(p_send, "xl", SWAP)
    q_send = pair_sum(half, 1 - my_zl, None).astype(BF16)
    q_got = lax.ppermute(q_send, "zl", SWAP)
    p_send = (pair_sum(0, 1 - my_zl, my_xl) + at(p_got, 1 - my_zl, 1).astype(F32)).astype(BF16)
    p_last = lax.ppermute(p_send, "zl", SWAP)
    q_got, _ = lax.optimization_barrier((q_got, p_send))
    q_send = (pair_sum(half, my_zl, 1 - my_xl) + at(q_got, 1 - my_xl, 1).astype(F32)).astype(BF16)
    q_last = lax.ppermute(q_send, "xl", SWAP)
    p_last, _ = lax.optimization_barrier((p_last, q_send))
    p = pair_sum(0, my_zl, my_xl) + at(p_got, my_zl, 1).astype(F32) + p_last.astype(F32)
    p = p.astype(BF16)
    q_last, _ = lax.optimization_barrier((q_last, p))
    q = pair_sum(half, my_zl, my_xl) + at(q_got, my_xl, 1).astype(F32) + q_last.astype(F32)
    q = q.astype(BF16)
    both = jnp.concatenate([p, q])
    both, blocks = lax.optimization_barrier((both, blocks))
    both = lax.all_to_all(both, "zh", 0, 0, tiled=True)
    grad_pair = jnp.sum(blocks, axis=0).reshape(-1, share, blocks.shape[2])
    my_xh = lax.axis_index("xh")
    grad_share = at(grad_pair, my_xh, 0) + lax.ppermute(at(grad_pair, 1 - my_xh, 0), "xh", SWAP)
    own_start = lax.axis_index("y") * pair + my_xh * share
    latent_share = lax.dynamic_slice_in_dim(latent_pre, own_start, share, 0)
    pre_share = norm_backward(latent_share, norm_gain, grad_share)
    both, pre_share = lax.optimization_barrier((both, pre_share))
    weight_grad = jnp.sum(both.astype(F32), axis=0)
    new_first = 0.9 * first_moment + 0.1 * weight_grad
    new_second = 0.999 * second_moment + 0.001 * weight_grad * weight_grad
    first_hat = new_first / bias_first
    second_hat = new_second / bias_second
    new_master = master - 0.01 * (first_hat / (jnp.sqrt(second_hat) + 1e-08) + 0.1 * master)
    rep = to_all(new_master.astype(BF16), "zh")
    pre_pair = gather_pair(pre_share, "xh", 0).reshape(pair, -1)
    rep, pre_pair = lax.optimization_barrier((rep, pre_pair))
    p = gather_pair(rep[:half], "zl", 1)
    q = gather_pair(rep[half:], "xl", 1)
    grad_pre = to_all(pre_pair, "y").reshape(latent_pre.shape)
    p = gather_pair(p, "xl", 2)
    q = gather_pair(q, "zl", 1)
    grad_hidden = lax.dot_general(
        grad_pre, down_weight, (((1,), (1,)), ((), ())), preferred_element_type=F32
    ).astype(BF16)
    new_replica = gather_pair(jnp.concatenate([p, q]), "c", 3).reshape(-1, cols)
    return (grad_hidden, new_master, new_first, new_second, new_replica)


def solution(mesh):
    torus = Mesh(mesh.devices.reshape(8, 2, 2, 2, 2, 8), ("zh", "zl", "xl", "c", "xh", "y"))
    placed = (
        P(DP, None),
        P(),
        P(None, TENSOR),
        P(TENSOR, None),
        P(DP, TENSOR),
        P(DP, TENSOR),
        P(DP, TENSOR),
        P(DP, TENSOR),
    )
    return jax.shard_map(
        local,
        mesh=torus,
        in_specs=placed,
        out_specs=(P(DP, TENSOR), P(DP, TENSOR), P(DP, TENSOR), P(DP, TENSOR), P(None, TENSOR)),
        check_vma=False,
    )
```
